32 devices in a mesh: pipe: 16 (over z, y, core), tensor: 2 (over x).
Axes of the slice: x: 2, y: 2, z: 4, core: 2. Of those that a mesh axis runs over, the one named last changes fastest.
Arguments:
- up_weight: bfloat16 [16, 6400, 3200], P('pipe', 'tensor'), may hold values from -0.109375 to 0.109375
- down_weight: bfloat16 [16, 6400, 3200], P('pipe', 'tensor'), may hold values from -0.078125 to 0.078125
- norm_gain: float32 [16, 3200], P('pipe'), may hold values from 0.1 to 1.9
- layer_scale: float32 [16, 3200], P('pipe'), may hold values from 0.25 to 1
- stash: bfloat16 [16, 3, 256, 3200], P('pipe', None, 'tensor'), may hold values from -6 to 6
- slot_order: int32 [16, 3], P('pipe'), may hold values from 0 to 2, each once within a row
- received: float32 [16, 256, 3200], P('pipe', 'tensor'), may hold values from -6 to 6
- arrivals: bfloat16 [3, 64, 12800], P(None, 'tensor'), may hold values from -6 to 6
Outputs:
- emitted: bfloat16 [16, 3, 256, 3200], P('pipe', None, 'tensor')
- pending: float32 [16, 256, 3200], P('pipe', 'tensor')
The draws below stay inside these ranges and needn't reach their ends.
Inputs may be any that keep to these rules, and one draw needn't show every extreme that they name: `slot_order`: each section's row is an ordering of the slots 0 to 2.
All inputs are finite; a program needn't handle non-finite values.
Results may differ from the reference program's by a relative error of at most 0.02.
Values may be sent and summed in bfloat16 or wider, within the bound.
A program may use at most 128 MiB of HBM per device.

```python
import math
import jax
import jax.numpy as jnp
from jax import lax

D = 3200
HID = 6400
GRID = 16
TICKS = 3
TOK = 256
SECTIONS = 16
N_TENSOR = 2


def block_levels(stream_key, shape, split, least, largest):
    factor_of = 1.0
    for axis_at, parts in split:
        draws = jax.random.uniform(jax.random.fold_in(jax.random.fold_in(stream_key, 6), axis_at), (parts,), jnp.float32, least / len(split), largest / len(split))
        factor_of = factor_of * jnp.repeat(jnp.exp(draws), shape[axis_at] // parts).reshape((-1,) + (1,) * (len(shape) - 1 - axis_at))
    return factor_of


def centred(key, shape, width, most, split=(), held_as=jnp.bfloat16):
    level = block_levels(key, shape, split, -0.22, 0.18) if split else 1.0
    array = jax.random.normal(key, shape, jnp.float32) * width * level
    return jnp.minimum(jnp.maximum(array, -most), most).astype(held_as)


def setup_inputs(seed: int = 0) -> dict:
    key_of = jax.random.split(jax.random.key(seed), 9)
    return {
        "up_weight": centred(key_of[0], (SECTIONS, HID, D), D ** -0.5, 0.109375, ((0, 16), (1, 2))),
        "down_weight": centred(key_of[1], (SECTIONS, HID, D), HID ** -0.5, 0.078125, ((0, 16), (1, 2))),
        "norm_gain": jnp.clip(1.0 + 0.18 * jax.random.normal(key_of[2], (SECTIONS, D), jnp.float32), 0.1, 1.9),
        "layer_scale": jnp.clip(jnp.exp(math.log(1.0) - 1.3862944 * jax.random.uniform(key_of[3], (SECTIONS, D), jnp.float32) ** block_levels(key_of[3], (SECTIONS, D), ((0, 16),), -0.2, 0.2)), 0.25, 1.0),
        "stash": centred(key_of[4], (SECTIONS, TICKS, TOK, D), 1.0, 6.0, ((0, 16), (2, 2))),
        "slot_order": jax.vmap(lambda own: jax.random.permutation(own, TICKS))(jax.random.split(key_of[5], SECTIONS)).reshape((SECTIONS, TICKS)).astype(jnp.int32),
        "received": centred(key_of[6], (SECTIONS, TOK, D), 1.0, 6.0, ((0, 16), (1, 2)), jnp.float32),
        "arrivals": centred(key_of[7], (TICKS, TOK // 4, 4 * D), 1.0, 6.0, ((1, 2),)),
    }


EPS = 1e-06

def gelu_slope(hidden):
    return 0.5 * (1.0 + jax.scipy.special.erf(hidden * 0.7071067811865476)) + hidden * jnp.exp(-0.5 * hidden * hidden) * 0.3989422804014327

def norm_parts(stash_rows):
    values = stash_rows.astype(jnp.float32)
    factor = lax.rsqrt(lax.optimization_barrier(jnp.mean(values * values, axis=-1, keepdims=True)) + EPS)
    return (factor, values * factor)

def recompute(stash_rows, gain, up_w, down_w, scaled):
    factor, normed = norm_parts(stash_rows)
    act = (normed * gain).astype(jnp.bfloat16)
    dims = (((1,), (1,)), ((), ()))
    hidden = lax.dot_general(act, up_w, dims, preferred_element_type=jnp.float32)
    upstream = lax.dot_general(scaled, down_w, dims, preferred_element_type=jnp.float32)
    return (upstream * gelu_slope(hidden)).astype(jnp.bfloat16)

def norm_back(stash_rows, gain, total):
    factor, normed = norm_parts(stash_rows)
    scaled_back = total * gain
    return factor * (scaled_back - normed * lax.optimization_barrier(jnp.mean(scaled_back * normed, axis=-1, keepdims=True)))

def reference(up_weight, down_weight, norm_gain, layer_scale, stash, slot_order, received, arrivals):
    half = GRID // 2
    landed = arrivals.reshape(TICKS, half, half, 2, 2, D).transpose(0, 1, 3, 2, 4, 5).reshape(TICKS, TOK, D).astype(jnp.float32)
    block = HID // N_TENSOR

    def section(item):
        up_w, down_w, gain, lscale, stash_rows, grads = item
        scaled = (grads * lscale).astype(jnp.bfloat16)
        slope = recompute(stash_rows, gain, up_w, down_w, scaled)
        total = jnp.zeros((TOK, D), jnp.float32)
        for k in range(N_TENSOR):
            part = jnp.dot(slope[:, k * block:(k + 1) * block], up_w[k * block:(k + 1) * block], preferred_element_type=jnp.float32)
            part = lax.optimization_barrier(part.astype(jnp.bfloat16)).astype(jnp.float32)
            total = total + part
        return grads + norm_back(stash_rows, gain, total)
    grads = received
    emitted = []
    section_ids = jnp.arange(SECTIONS, dtype=jnp.int32)
    for tick in range(TICKS):
        chosen = stash[section_ids, slot_order[:, tick].astype(jnp.int32)]
        moved = lax.map(section, (up_weight, down_weight, norm_gain, layer_scale, chosen, grads))
        emitted.append(moved.astype(jnp.bfloat16))
        grads = jnp.concatenate([moved[1:], landed[tick][None]], axis=0)
    return (jnp.stack(emitted, axis=1), grads)
```

```python
import functools

import jax
import jax.numpy as jnp
from jax import lax
from jax.experimental import pallas as pl
from jax.experimental.pallas import tpu as pltpu
from jax.sharding import PartitionSpec as P

GRID = 16
EPS = 1e-06
CHUNKS = 4
RING = 4
TILE = 512
MESH = pl.DeviceIdType.MESH
NT = (((1,), (1,)), ((), ()))


def gelu_slope(hidden):
    return (
        0.5 * (1.0 + lax.erf(hidden * 0.7071067811865476))
        + hidden * jnp.exp(-0.5 * hidden * hidden) * 0.3989422804014327
    )


def tiles_of(size):
    return size // TILE, size % TILE


def kernel(
    n, sections, steps, order, gain, lscale, up_hbm, down_hbm, stash_hbm, received_hbm, landed_hbm,
    out_hbm, pend_hbm,
    up_w, down_w, stash, grads, landed, act, scaled, slope, psend, precv, gin, moved_b,
    wsem, isem, a_send, a_recv, s_send, s_recv, p_send, p_recv, g_send, g_recv, o_sem, e_sem,
):
    hid, width = up_w.shape
    rows = grads.shape[1]
    me = lax.axis_index("tensor")
    sec = lax.axis_index("pipe")
    has_next = sec > 0
    has_prev = sec < sections - 1
    is_last = sec == sections - 1
    full, rem = tiles_of(hid)
    wfull, wrem = tiles_of(width)

    def peer(d):
        return lax.rem(me + d, n)

    in_stash = pltpu.make_async_copy(stash_hbm, stash, isem.at[0])
    in_grads = pltpu.make_async_copy(received_hbm, grads, isem.at[1])
    in_landed = pltpu.make_async_copy(landed_hbm, landed, isem.at[2])
    in_stash.start()
    in_grads.start()

    def weight_copies(j, size):
        first = j * TILE
        if not isinstance(j, int):
            first = pl.multiple_of(first, TILE)
        span = pl.ds(first, size)
        return (
            pltpu.make_async_copy(up_hbm.at[span], up_w.at[span], wsem.at[0, j]),
            pltpu.make_async_copy(down_hbm.at[span], down_w.at[span], wsem.at[1, j]),
        )

    for j in range(full + (rem > 0)):
        for copy in weight_copies(j, TILE if j < full else rem):
            copy.start()
    in_landed.start()

    barrier = pltpu.get_barrier_semaphore()
    for d in range(1, n):
        pl.semaphore_signal(barrier, inc=1, device_id={"tensor": peer(d)}, device_id_type=MESH)

    @pl.when(has_next)
    def _():
        pl.semaphore_signal(barrier, inc=1, device_id={"pipe": sec - 1}, device_id_type=MESH)

    @pl.when(has_prev)
    def _():
        pl.semaphore_signal(barrier, inc=1, device_id={"pipe": sec + 1}, device_id_type=MESH)

    def stash_rows(q):
        tick, chunk = q // CHUNKS, q % CHUNKS
        values = stash[order[0, tick], chunk].astype(jnp.float32)
        factor = lax.rsqrt(jnp.mean(values * values, axis=-1, keepdims=True) + EPS)
        return factor, values * factor

    def spread(buf, send, recv, slot, d):
        return pltpu.make_async_remote_copy(
            src_ref=buf.at[slot, me],
            dst_ref=buf.at[slot, me],
            send_sem=send.at[slot, d - 1],
            recv_sem=recv.at[slot, d - 1],
            device_id={"tensor": peer(d)},
            device_id_type=MESH,
        )

    def part_copy(slot, d):
        return pltpu.make_async_remote_copy(
            src_ref=psend.at[slot, peer(d)],
            dst_ref=precv.at[slot, d - 1],
            send_sem=p_send.at[slot, d - 1],
            recv_sem=p_recv.at[slot, d - 1],
            device_id={"tensor": peer(d)},
            device_id_type=MESH,
        )

    def pipe_copy(q):
        return pltpu.make_async_remote_copy(
            src_ref=moved_b.at[q],
            dst_ref=gin.at[q],
            send_sem=g_send.at[q],
            recv_sem=g_recv.at[q],
            device_id={"pipe": jnp.maximum(sec - 1, 0)},
            device_id_type=MESH,
        )

    def out_copy(q):
        return pltpu.make_async_copy(moved_b.at[q], out_hbm.at[q], o_sem.at[q])

    def send_act(q):
        slot = q % RING
        _, normed = stash_rows(q)
        act[slot, me] = (normed * gain[...]).astype(jnp.bfloat16)
        for d in range(1, n):
            spread(act, a_send, a_recv, slot, d).start()

    def send_scaled(q):
        slot = q % RING
        scaled[slot, me] = (grads[q % CHUNKS] * lscale[...]).astype(jnp.bfloat16)
        for d in range(1, n):
            spread(scaled, s_send, s_recv, slot, d).start()

    def finish(q):
        slot, chunk = q % RING, q % CHUNKS
        for d in range(1, n):
            part_copy(slot, d).wait_recv()
        total = psend[slot, me].astype(jnp.float32)
        for d in range(1, n):
            total += precv[slot, d - 1].astype(jnp.float32)
        factor, normed = stash_rows(q)
        back = total * gain[...]
        moved = grads[chunk] + factor * (back - normed * jnp.mean(back * normed, axis=-1, keepdims=True))
        moved_b[q] = moved.astype(jnp.bfloat16)

        @pl.when(has_next)
        def _():
            pipe_copy(q).start()

        out_copy(q).start()

    def next_grads(q):
        chunk, before = q % CHUNKS, q - CHUNKS

        @pl.when(is_last)
        def _():
            grads[chunk] = landed[before].astype(jnp.float32)

        @pl.when(has_prev)
        def _():
            pipe_copy(before).wait_recv()
            grads[chunk] = gin[before].astype(jnp.float32)

    in_stash.wait()
    in_grads.wait()
    heads = min(2, steps)
    for q in range(heads):
        slot = q % RING
        _, normed = stash_rows(q)
        act[slot, me] = (normed * gain[...]).astype(jnp.bfloat16)
        scaled[slot, me] = (grads[q % CHUNKS] * lscale[...]).astype(jnp.bfloat16)
        if q == 0:
            waits = (n - 1) + has_next.astype(jnp.int32) + has_prev.astype(jnp.int32)
            pl.semaphore_wait(barrier, waits)
        for d in range(1, n):
            spread(act, a_send, a_recv, slot, d).start()
        for d in range(1, n):
            spread(scaled, s_send, s_recv, slot, d).start()
    in_landed.wait()

    tokens = n * rows

    def step(q, carry):
        slot = q % RING
        for d in range(1, n):
            spread(act, a_send, a_recv, slot, d).wait_recv()
            spread(scaled, s_send, s_recv, slot, d).wait_recv()

        def up_tile(j, size):
            @pl.when(q == 0)
            def _():
                for copy in weight_copies(j, size):
                    copy.wait()

            first = j * TILE
            if not isinstance(j, int):
                first = pl.multiple_of(first, TILE)
            span = pl.ds(first, size)
            hidden = lax.dot_general(
                act[slot].reshape(tokens, width), up_w[span, :], NT, preferred_element_type=jnp.float32
            )
            upstream = lax.dot_general(
                scaled[slot].reshape(tokens, width), down_w[span, :], NT, preferred_element_type=jnp.float32
            )
            slope[:, span] = (upstream * gelu_slope(hidden)).astype(jnp.bfloat16)

        pl.loop(0, full)(lambda j: up_tile(j, TILE))
        if rem:
            up_tile(full, rem)

        @pl.when(q >= RING)
        def _():
            for d in range(1, n):
                part_copy(slot, d).wait_send()

        def down_tile(j, size):
            first = j * TILE
            if not isinstance(j, int):
                first = pl.multiple_of(first, TILE)
            span = pl.ds(first, size)
            part = jnp.dot(slope[...], up_w[:, span], preferred_element_type=jnp.float32)
            psend[slot, :, :, span] = part.astype(jnp.bfloat16).reshape(n, rows, size)

        pl.loop(0, wfull)(lambda j: down_tile(j, TILE))
        if wrem:
            down_tile(wfull, wrem)
        for d in range(1, n):
            part_copy(slot, d).start()

        @pl.when(q >= 1)
        def _():
            finish(q - 1)

        @pl.when(q + heads < steps)
        def _():
            later = q + heads

            @pl.when(later >= RING)
            def _():
                for d in range(1, n):
                    spread(act, a_send, a_recv, later % RING, d).wait_send()
                    spread(scaled, s_send, s_recv, later % RING, d).wait_send()

            @pl.when(later >= CHUNKS)
            def _():
                next_grads(later)

            send_scaled(later)
            send_act(later)

        return carry

    lax.fori_loop(0, steps, step, 0)
    finish(steps - 1)

    for q in range(steps - CHUNKS, steps):
        @pl.when(has_prev)
        def _(q=q):
            pipe_copy(q).wait_recv()
            pltpu.make_async_copy(gin.at[q], pend_hbm.at[q - steps + CHUNKS], e_sem.at[q - steps + CHUNKS]).start()

    for q in range(steps):
        out_copy(q).wait()

        @pl.when(has_next)
        def _(q=q):
            pipe_copy(q).wait_send()

    for slot in range(min(RING, steps)):
        for d in range(1, n):
            spread(act, a_send, a_recv, slot, d).wait_send()
            spread(scaled, s_send, s_recv, slot, d).wait_send()
            part_copy(slot, d).wait_send()
    for c in range(CHUNKS):
        @pl.when(has_prev)
        def _(c=c):
            pltpu.make_async_copy(gin.at[steps - CHUNKS + c], pend_hbm.at[c], e_sem.at[c]).wait()


def shards(n, sections, up_weight, down_weight, norm_gain, layer_scale, stash, slot_order, received, arrivals):
    up_w, down_w = up_weight[0], down_weight[0]
    hid, width = up_w.shape
    _, ticks, tokens, _ = stash.shape
    half = GRID // 2
    lines = tokens // 4 // half
    rows = tokens // CHUNKS
    steps = ticks * CHUNKS
    landed = (
        arrivals.reshape(ticks, lines, half, 2, 2, width)
        .transpose(0, 1, 3, 2, 4, 5)
        .reshape(ticks, tokens, width)
    )
    bf = jnp.bfloat16
    hold = pl.BlockSpec(memory_space=pltpu.VMEM)
    far = pl.BlockSpec(memory_space=pl.ANY)
    dma = pltpu.SemaphoreType.DMA
    tile_count = hid // TILE + (hid % TILE > 0)
    out, pend = pl.pallas_call(
        functools.partial(kernel, n, sections, steps),
        out_shape=(
            jax.ShapeDtypeStruct((steps, rows, width), bf),
            jax.ShapeDtypeStruct((CHUNKS, rows, width), bf),
        ),
        in_specs=[pl.BlockSpec(memory_space=pltpu.SMEM), hold, hold, far, far, far, far, far],
        out_specs=(far, far),
        scratch_shapes=[
            pltpu.VMEM((hid, width), bf),
            pltpu.VMEM((hid, width), bf),
            pltpu.VMEM((ticks, CHUNKS, rows, width), bf),
            pltpu.VMEM((CHUNKS, rows, width), jnp.float32),
            pltpu.VMEM((steps, rows, width), bf),
            pltpu.VMEM((RING, n, rows, width), bf),
            pltpu.VMEM((RING, n, rows, width), bf),
            pltpu.VMEM((n * rows, hid), bf),
            pltpu.VMEM((RING, n, rows, width), bf),
            pltpu.VMEM((RING, n - 1, rows, width), bf),
            pltpu.VMEM((steps, rows, width), bf),
            pltpu.VMEM((steps, rows, width), bf),
            dma((2, tile_count)),
            dma((3,)),
            dma((RING, n - 1)),
            dma((RING, n - 1)),
            dma((RING, n - 1)),
            dma((RING, n - 1)),
            dma((RING, n - 1)),
            dma((RING, n - 1)),
            dma((steps,)),
            dma((steps,)),
            dma((steps,)),
            dma((CHUNKS,)),
        ],
        compiler_params=pltpu.CompilerParams(
            collective_id=0, has_side_effects=True, vmem_limit_bytes=66 * 1024 * 1024 - 2 * 1024 * 1024
        ),
    )(
        slot_order,
        norm_gain,
        layer_scale,
        up_w,
        down_w,
        stash.reshape(ticks, CHUNKS, rows, width),
        received.reshape(CHUNKS, rows, width),
        landed.reshape(steps, rows, width),
    )
    is_last = lax.axis_index("pipe") == sections - 1
    pending = jnp.where(is_last, landed[ticks - 1], pend.reshape(tokens, width)).astype(jnp.float32)
    return out.reshape(1, ticks, tokens, width), pending[None]


def solution(mesh):
    return jax.shard_map(
        functools.partial(shards, mesh.shape["tensor"], mesh.shape["pipe"]),
        mesh=mesh,
        in_specs=(
            P("pipe", "tensor", None),
            P("pipe", "tensor", None),
            P("pipe", None),
            P("pipe", None),
            P("pipe", None, "tensor", None),
            P("pipe", None),
            P("pipe", "tensor", None),
            P(None, "tensor", None),
        ),
        out_specs=(P("pipe", None, "tensor", None), P("pipe", "tensor", None)),
        check_vma=False,
    )
```

```python
import functools

import jax
import jax.numpy as jnp
from jax import lax
from jax.experimental import pallas as pl
from jax.experimental.pallas import tpu as pltpu
from jax.sharding import PartitionSpec as P

GRID = 16
EPS = 1e-06
CHUNKS = 2
RING = 2
HELD = 2 * CHUNKS
TILE = 512
MESH = pl.DeviceIdType.MESH
NT = (((1,), (1,)), ((), ()))


def gelu_slope(hidden):
    return (
        0.5 * (1.0 + lax.erf(hidden * 0.7071067811865476))
        + hidden * jnp.exp(-0.5 * hidden * hidden) * 0.3989422804014327
    )


def tiles_of(size):
    return size // TILE, size % TILE


def kernel(
    n, sections, steps, order, gain, lscale, up_hbm, down_hbm, stash_hbm, received_hbm, landed_hbm,
    out_hbm, pend_hbm,
    up_w, down_w, stash, grads, landed, act, scaled, factor_of, slope, psend, precv, gin, moved_b,
    wsem, isem, a_send, a_recv, s_send, s_recv, p_send, p_recv, g_send, g_recv, o_sem, e_sem,
):
    hid, width = up_w.shape
    rows = grads.shape[1]
    me = lax.axis_index("tensor")
    sec = lax.axis_index("pipe")
    has_next = sec > 0
    has_prev = sec < sections - 1
    is_last = sec == sections - 1
    full, rem = tiles_of(hid)
    wfull, wrem = tiles_of(width)

    def peer(d):
        return lax.rem(me + d, n)

    in_stash = pltpu.make_async_copy(stash_hbm, stash, isem.at[0])
    in_grads = pltpu.make_async_copy(received_hbm, grads, isem.at[1])
    in_landed = pltpu.make_async_copy(landed_hbm, landed, isem.at[2])
    in_stash.start()
    in_grads.start()

    def weight_copies(j, size):
        first = j * TILE
        if not isinstance(j, int):
            first = pl.multiple_of(first, TILE)
        span = pl.ds(first, size)
        return (
            pltpu.make_async_copy(up_hbm.at[span], up_w.at[span], wsem.at[0, j]),
            pltpu.make_async_copy(down_hbm.at[span], down_w.at[span], wsem.at[1, j]),
        )

    for which in range(2):
        for j in range(full + (rem > 0)):
            weight_copies(j, TILE if j < full else rem)[which].start()
    in_landed.start()

    barrier = pltpu.get_barrier_semaphore()
    for d in range(1, n):
        pl.semaphore_signal(barrier, inc=1, device_id={"tensor": peer(d)}, device_id_type=MESH)

    @pl.when(has_next)
    def _():
        pl.semaphore_signal(barrier, inc=1, device_id={"pipe": sec - 1}, device_id_type=MESH)

    @pl.when(has_prev)
    def _():
        pl.semaphore_signal(barrier, inc=1, device_id={"pipe": sec + 1}, device_id_type=MESH)

    def stash_rows(q):
        tick, chunk = q // CHUNKS, q % CHUNKS
        values = stash[order[0, tick], chunk].astype(jnp.float32)
        factor = lax.rsqrt(jnp.mean(values * values, axis=-1, keepdims=True) + EPS)
        return factor, values * factor

    def spread(buf, send, recv, slot, d):
        return pltpu.make_async_remote_copy(
            src_ref=buf.at[slot, me],
            dst_ref=buf.at[slot, me],
            send_sem=send.at[slot, d - 1],
            recv_sem=recv.at[slot, d - 1],
            device_id={"tensor": peer(d)},
            device_id_type=MESH,
        )

    def part_copy(slot, d, span=slice(None)):
        return pltpu.make_async_remote_copy(
            src_ref=psend.at[slot, peer(d), :, span],
            dst_ref=precv.at[slot, d - 1, :, span],
            send_sem=p_send.at[slot, d - 1],
            recv_sem=p_recv.at[slot, d - 1],
            device_id={"tensor": peer(d)},
            device_id_type=MESH,
        )

    def pipe_copy(q):
        return pltpu.make_async_remote_copy(
            src_ref=moved_b.at[q],
            dst_ref=gin.at[q],
            send_sem=g_send.at[q],
            recv_sem=g_recv.at[q],
            device_id={"pipe": jnp.maximum(sec - 1, 0)},
            device_id_type=MESH,
        )

    def out_copy(q):
        return pltpu.make_async_copy(moved_b.at[q], out_hbm.at[q], o_sem.at[q])

    def act_copy(a, d):
        return spread(act, a_send, a_recv, a % HELD, d)

    def make_act(a):
        _, normed = stash_rows(a)
        act[a % HELD, me] = (normed * gain[...]).astype(jnp.bfloat16)

    def make_scaled(q):
        scaled[q % RING, me] = (grads[q % CHUNKS] * lscale[...]).astype(jnp.bfloat16)

    def scaled_copy(q, d):
        return spread(scaled, s_send, s_recv, q % RING, d)

    def finish(q):
        slot, chunk = q % RING, q % CHUNKS
        for d in range(1, n):
            part_copy(slot, d).wait_recv()
        total = psend[slot, me].astype(jnp.float32)
        for d in range(1, n):
            total += precv[slot, d - 1].astype(jnp.float32)
        factor, normed = stash_rows(q)
        back = total * gain[...]
        moved = grads[chunk] + factor * (back - normed * jnp.mean(back * normed, axis=-1, keepdims=True))
        moved_b[q] = moved.astype(jnp.bfloat16)

        @pl.when(has_next)
        def _():
            pipe_copy(q).start()

        out_copy(q).start()

    def next_grads(q):
        chunk, before = q % CHUNKS, q - CHUNKS

        @pl.when(is_last)
        def _():
            grads[chunk] = landed[before].astype(jnp.float32)

        @pl.when(has_prev)
        def _():
            pipe_copy(before).wait_recv()
            grads[chunk] = gin[before].astype(jnp.float32)

    in_stash.wait()
    in_grads.wait()
    for a in range(CHUNKS):
        make_act(a)
        if a == 0:
            waits = (n - 1) + has_next.astype(jnp.int32) + has_prev.astype(jnp.int32)
            pl.semaphore_wait(barrier, waits)
        for d in range(1, n):
            act_copy(a, d).start()
    for q in range(CHUNKS):
        make_scaled(q)
        for d in range(1, n):
            scaled_copy(q, d).start()
    ahead = min(CHUNKS + 1, steps)
    for a in range(CHUNKS, ahead):
        make_act(a)
        for d in range(1, n):
            act_copy(a, d).start()
    in_landed.wait()

    tokens = n * rows

    def aligned(j):
        first = j * TILE
        return first if isinstance(j, int) else pl.multiple_of(first, TILE)

    def step(q, carry):
        slot, chunk = q % RING, q % CHUNKS

        def arrive(which, j, size):
            @pl.when(q == 0)
            def _():
                weight_copies(j, size)[which].wait()

        def hidden_tile(j, size):
            arrive(0, j, size)
            span = pl.ds(aligned(j), size)
            rows_of = act[pl.ds(q % HELD, CHUNKS)].reshape(CHUNKS * tokens, width)
            hidden = lax.dot_general(rows_of, up_w[span, :], NT, preferred_element_type=jnp.float32)
            factor_of[:, :, span] = gelu_slope(hidden).reshape(CHUNKS, tokens, size)

        @pl.when(chunk == 0)
        def _():
            for c in range(CHUNKS):
                for d in range(1, n):
                    act_copy(q + c, d).wait_recv()
            pl.loop(0, full)(lambda j: hidden_tile(j, TILE))
            if rem:
                hidden_tile(full, rem)

        for d in range(1, n):
            scaled_copy(q, d).wait_recv()

        def up_tile(j, size):
            arrive(1, j, size)
            span = pl.ds(aligned(j), size)
            upstream = lax.dot_general(
                scaled[slot].reshape(tokens, width), down_w[span, :], NT, preferred_element_type=jnp.float32
            )
            slope[:, span] = (upstream * factor_of[chunk, :, span]).astype(jnp.bfloat16)

        pl.loop(0, full)(lambda j: up_tile(j, TILE))
        if rem:
            up_tile(full, rem)

        @pl.when(q >= 1)
        def _():
            finish(q - 1)

        @pl.when(q >= RING)
        def _():
            for d in range(1, n):
                part_copy(slot, d).wait_send()

        def down_tile(j, size):
            span = pl.ds(aligned(j), size)
            part = jnp.dot(slope[...], up_w[:, span], preferred_element_type=jnp.float32)
            psend[slot, :, :, span] = part.astype(jnp.bfloat16).reshape(n, rows, size)
            for d in range(1, n):
                part_copy(slot, d, span).start()

        pl.loop(0, wfull)(lambda j: down_tile(j, TILE))
        if wrem:
            down_tile(wfull, wrem)

        @pl.when((q + 1 >= CHUNKS) & (q + 1 < steps))
        def _():
            for d in range(1, n):
                scaled_copy(q + 1, d).wait_send()
            next_grads(q + 1)
            make_scaled(q + 1)
            for d in range(1, n):
                scaled_copy(q + 1, d).start()

        @pl.when(q + ahead < steps)
        def _():
            later = q + ahead

            @pl.when(later >= HELD)
            def _():
                for d in range(1, n):
                    act_copy(later, d).wait_send()

            make_act(later)
            for d in range(1, n):
                act_copy(later, d).start()

        return carry

    lax.fori_loop(0, steps, step, 0)
    finish(steps - 1)

    for q in range(steps - CHUNKS, steps):
        @pl.when(has_prev)
        def _(q=q):
            pipe_copy(q).wait_recv()
            pltpu.make_async_copy(gin.at[q], pend_hbm.at[q - steps + CHUNKS], e_sem.at[q - steps + CHUNKS]).start()

    for q in range(steps):
        out_copy(q).wait()

        @pl.when(has_next)
        def _(q=q):
            pipe_copy(q).wait_send()

    for d in range(1, n):
        for slot in range(RING):
            scaled_copy(slot, d).wait_send()
            part_copy(slot, d).wait_send()
        for slot in range(min(HELD, steps)):
            act_copy(slot, d).wait_send()
    for c in range(CHUNKS):
        @pl.when(has_prev)
        def _(c=c):
            pltpu.make_async_copy(gin.at[steps - CHUNKS + c], pend_hbm.at[c], e_sem.at[c]).wait()


def shards(n, sections, up_weight, down_weight, norm_gain, layer_scale, stash, slot_order, received, arrivals):
    up_w, down_w = up_weight[0], down_weight[0]
    hid, width = up_w.shape
    _, ticks, tokens, _ = stash.shape
    half = GRID // 2
    lines = tokens // 4 // half
    rows = tokens // CHUNKS
    steps = ticks * CHUNKS
    landed = (
        arrivals.reshape(ticks, lines, half, 2, 2, width)
        .transpose(0, 1, 3, 2, 4, 5)
        .reshape(ticks, tokens, width)
    )
    bf = jnp.bfloat16
    hold = pl.BlockSpec(memory_space=pltpu.VMEM)
    far = pl.BlockSpec(memory_space=pl.ANY)
    dma = pltpu.SemaphoreType.DMA
    tile_count = hid // TILE + (hid % TILE > 0)
    out, pend = pl.pallas_call(
        functools.partial(kernel, n, sections, steps),
        out_shape=(
            jax.ShapeDtypeStruct((steps, rows, width), bf),
            jax.ShapeDtypeStruct((CHUNKS, rows, width), bf),
        ),
        in_specs=[pl.BlockSpec(memory_space=pltpu.SMEM), hold, hold, far, far, far, far, far],
        out_specs=(far, far),
        scratch_shapes=[
            pltpu.VMEM((hid, width), bf),
            pltpu.VMEM((hid, width), bf),
            pltpu.VMEM((ticks, CHUNKS, rows, width), bf),
            pltpu.VMEM((CHUNKS, rows, width), jnp.float32),
            pltpu.VMEM((steps - CHUNKS, rows, width), bf),
            pltpu.VMEM((HELD, n, rows, width), bf),
            pltpu.VMEM((RING, n, rows, width), bf),
            pltpu.VMEM((CHUNKS, n * rows, hid), jnp.float32),
            pltpu.VMEM((n * rows, hid), bf),
            pltpu.VMEM((RING, n, rows, width), bf),
            pltpu.VMEM((RING, n - 1, rows, width), bf),
            pltpu.VMEM((steps, rows, width), bf),
            pltpu.VMEM((steps, rows, width), bf),
            dma((2, tile_count)),
            dma((3,)),
            dma((HELD, n - 1)),
            dma((HELD, n - 1)),
            dma((RING, n - 1)),
            dma((RING, n - 1)),
            dma((RING, n - 1)),
            dma((RING, n - 1)),
            dma((steps,)),
            dma((steps,)),
            dma((steps,)),
            dma((CHUNKS,)),
        ],
        compiler_params=pltpu.CompilerParams(
            collective_id=0, has_side_effects=True, vmem_limit_bytes=67_043_328
        ),
    )(
        slot_order,
        norm_gain,
        layer_scale,
        up_w,
        down_w,
        stash.reshape(ticks, CHUNKS, rows, width),
        received.reshape(CHUNKS, rows, width),
        landed[: ticks - 1].reshape(steps - CHUNKS, rows, width),
    )
    is_last = lax.axis_index("pipe") == sections - 1
    pending = jnp.where(is_last, landed[ticks - 1], pend.reshape(tokens, width)).astype(jnp.float32)
    return out.reshape(1, ticks, tokens, width), pending[None]


def solution(mesh):
    return jax.shard_map(
        functools.partial(shards, mesh.shape["tensor"], mesh.shape["pipe"]),
        mesh=mesh,
        in_specs=(
            P("pipe", "tensor", None),
            P("pipe", "tensor", None),
            P("pipe", None),
            P("pipe", None),
            P("pipe", None, "tensor", None),
            P("pipe", None),
            P("pipe", "tensor", None),
            P(None, "tensor", None),
        ),
        out_specs=(P("pipe", None, "tensor", None), P("pipe", "tensor", None)),
        check_vma=False,
    )
```

```python
import functools

import jax
import jax.numpy as jnp
from jax import lax
from jax.experimental import pallas as pl
from jax.experimental.pallas import tpu as pltpu
from jax.sharding import PartitionSpec as P

GRID = 16
EPS = 1e-06
CHUNKS = 2
RING = CHUNKS
HELD = 2 * CHUNKS
TILE = 512
MESH = pl.DeviceIdType.MESH
NT = (((1,), (1,)), ((), ()))


def gelu_slope(hidden):
    return (
        0.5 * (1.0 + lax.erf(hidden * 0.7071067811865476))
        + hidden * jnp.exp(-0.5 * hidden * hidden) * 0.3989422804014327
    )


def tiles_of(size):
    return size // TILE, size % TILE


def kernel(
    n, sections, steps, order, gain, lscale, up_hbm, down_hbm, stash_hbm, received_hbm, landed_hbm,
    out_hbm, pend_hbm,
    up_w, down_w, stash, grads, landed, act, scaled, factor_of, slope, psend, precv, gin, moved_b,
    wsem, isem, a_send, a_recv, s_send, s_recv, p_send, p_recv, g_send, g_recv, o_sem, e_sem,
):
    hid, width = up_w.shape
    rows = grads.shape[1]
    me = lax.axis_index("tensor")
    sec = lax.axis_index("pipe")
    has_next = sec > 0
    has_prev = sec < sections - 1
    is_last = sec == sections - 1
    full, rem = tiles_of(hid)
    wfull, wrem = tiles_of(width)

    def peer(d):
        return lax.rem(me + d, n)

    in_stash = pltpu.make_async_copy(stash_hbm, stash, isem.at[0])
    in_grads = pltpu.make_async_copy(received_hbm, grads, isem.at[1])
    in_landed = pltpu.make_async_copy(landed_hbm, landed, isem.at[2])
    in_stash.start()
    in_grads.start()

    def weight_copies(j, size):
        first = j * TILE
        if not isinstance(j, int):
            first = pl.multiple_of(first, TILE)
        span = pl.ds(first, size)
        return (
            pltpu.make_async_copy(up_hbm.at[span], up_w.at[span], wsem.at[0, j]),
            pltpu.make_async_copy(down_hbm.at[span], down_w.at[span], wsem.at[1, j]),
        )

    for which in range(2):
        for j in range(full + (rem > 0)):
            weight_copies(j, TILE if j < full else rem)[which].start()
    in_landed.start()

    barrier = pltpu.get_barrier_semaphore()
    for d in range(1, n):
        pl.semaphore_signal(barrier, inc=1, device_id={"tensor": peer(d)}, device_id_type=MESH)

    @pl.when(has_next)
    def _():
        pl.semaphore_signal(barrier, inc=1, device_id={"pipe": sec - 1}, device_id_type=MESH)

    @pl.when(has_prev)
    def _():
        pl.semaphore_signal(barrier, inc=1, device_id={"pipe": sec + 1}, device_id_type=MESH)

    def stash_rows(q):
        tick, chunk = q // CHUNKS, q % CHUNKS
        values = stash[order[0, tick], chunk].astype(jnp.float32)
        factor = lax.rsqrt(jnp.mean(values * values, axis=-1, keepdims=True) + EPS)
        return factor, values * factor

    def spread(buf, send, recv, slot, d):
        return pltpu.make_async_remote_copy(
            src_ref=buf.at[slot, me],
            dst_ref=buf.at[slot, me],
            send_sem=send.at[slot, d - 1],
            recv_sem=recv.at[slot, d - 1],
            device_id={"tensor": peer(d)},
            device_id_type=MESH,
        )

    def part_copy(slot, d, span=slice(None)):
        return pltpu.make_async_remote_copy(
            src_ref=psend.at[slot, peer(d), :, span],
            dst_ref=precv.at[slot, d - 1, :, span],
            send_sem=p_send.at[slot, d - 1],
            recv_sem=p_recv.at[slot, d - 1],
            device_id={"tensor": peer(d)},
            device_id_type=MESH,
        )

    def pipe_copy(q):
        return pltpu.make_async_remote_copy(
            src_ref=moved_b.at[q],
            dst_ref=gin.at[q],
            send_sem=g_send.at[q],
            recv_sem=g_recv.at[q],
            device_id={"pipe": jnp.maximum(sec - 1, 0)},
            device_id_type=MESH,
        )

    def out_copy(q):
        return pltpu.make_async_copy(moved_b.at[q], out_hbm.at[q], o_sem.at[q])

    def act_copy(a, d):
        return spread(act, a_send, a_recv, a % HELD, d)

    def make_act(a):
        _, normed = stash_rows(a)
        act[a % HELD, me] = (normed * gain[...]).astype(jnp.bfloat16)

    def make_scaled(q):
        scaled[q % RING, me] = (grads[q % CHUNKS] * lscale[...]).astype(jnp.bfloat16)

    def scaled_copy(q, d):
        return spread(scaled, s_send, s_recv, q % RING, d)

    def finish(q):
        slot, chunk = q % RING, q % CHUNKS
        for d in range(1, n):
            part_copy(slot, d).wait_recv()
        total = psend[slot, me].astype(jnp.float32)
        for d in range(1, n):
            total += precv[slot, d - 1].astype(jnp.float32)
        factor, normed = stash_rows(q)
        back = total * gain[...]
        moved = grads[chunk] + factor * (back - normed * jnp.mean(back * normed, axis=-1, keepdims=True))
        moved_b[q] = moved.astype(jnp.bfloat16)

        @pl.when(has_next)
        def _():
            pipe_copy(q).start()

        out_copy(q).start()

    def next_grads(q):
        chunk, before = q % CHUNKS, q - CHUNKS

        @pl.when(is_last)
        def _():
            grads[chunk] = landed[before].astype(jnp.float32)

        @pl.when(has_prev)
        def _():
            pipe_copy(before).wait_recv()
            grads[chunk] = gin[before].astype(jnp.float32)

    in_stash.wait()
    in_grads.wait()
    for a in range(CHUNKS):
        make_act(a)
        if a == 0:
            waits = (n - 1) + has_next.astype(jnp.int32) + has_prev.astype(jnp.int32)
            pl.semaphore_wait(barrier, waits)
        for d in range(1, n):
            act_copy(a, d).start()
    for q in range(CHUNKS):
        make_scaled(q)
        for d in range(1, n):
            scaled_copy(q, d).start()
    in_landed.wait()

    tokens = n * rows

    def aligned(j):
        first = j * TILE
        return first if isinstance(j, int) else pl.multiple_of(first, TILE)

    ticks = steps // CHUNKS

    def send_act(a):
        @pl.when(a >= HELD)
        def _():
            for d in range(1, n):
                act_copy(a, d).wait_send()

        make_act(a)
        for d in range(1, n):
            act_copy(a, d).start()

    def send_next(q):
        for d in range(1, n):
            scaled_copy(q, d).wait_send()
        next_grads(q)
        make_scaled(q)
        for d in range(1, n):
            scaled_copy(q, d).start()

    def tick_of(tick, carry):
        head = tick * CHUNKS
        more = tick + 1 < ticks

        def arrive(which, j, size):
            @pl.when(tick == 0)
            def _():
                weight_copies(j, size)[which].wait()

        def hidden_tile(j, size):
            arrive(0, j, size)
            span = pl.ds(aligned(j), size)
            rows_of = act[pl.ds(head % HELD, CHUNKS)].reshape(CHUNKS * tokens, width)
            hidden = lax.dot_general(rows_of, up_w[span, :], NT, preferred_element_type=jnp.float32)
            factor_of[:, :, span] = gelu_slope(hidden).reshape(CHUNKS, tokens, size)

        for c in range(CHUNKS):
            for d in range(1, n):
                act_copy(head + c, d).wait_recv()
        pl.loop(0, full)(lambda j: hidden_tile(j, TILE))
        if rem:
            hidden_tile(full, rem)

        @pl.when(tick >= 1)
        def _():
            send_next(head + CHUNKS - 1)

        @pl.when(more)
        def _():
            send_act(head + CHUNKS)

        for c in range(CHUNKS):
            q = head + c
            for d in range(1, n):
                scaled_copy(q, d).wait_recv()

            def up_tile(j, size):
                if c == 0:
                    arrive(1, j, size)
                span = pl.ds(aligned(j), size)
                upstream = lax.dot_general(
                    scaled[c].reshape(tokens, width), down_w[span, :], NT, preferred_element_type=jnp.float32
                )
                slope[:, span] = (upstream * factor_of[c, :, span]).astype(jnp.bfloat16)

            pl.loop(0, full)(lambda j: up_tile(j, TILE))
            if rem:
                up_tile(full, rem)
            if c:
                finish(q - 1)

            @pl.when(tick >= 1)
            def _():
                for d in range(1, n):
                    part_copy(c, d).wait_send()

            def down_tile(j, size):
                span = pl.ds(aligned(j), size)
                part = jnp.dot(slope[...], up_w[:, span], preferred_element_type=jnp.float32)
                psend[c, :, :, span] = part.astype(jnp.bfloat16).reshape(n, rows, size)
                for d in range(1, n):
                    part_copy(c, d, span).start()

            pl.loop(0, wfull)(lambda j: down_tile(j, TILE))
            if wrem:
                down_tile(wfull, wrem)

            @pl.when(more)
            def _():
                if c:
                    send_next(q - 1 + CHUNKS)
                if c + 1 < CHUNKS:
                    send_act(q + 1 + CHUNKS)

        finish(head + CHUNKS - 1)
        return carry

    lax.fori_loop(0, ticks, tick_of, 0)

    for q in range(steps - CHUNKS, steps):
        @pl.when(has_prev)
        def _(q=q):
            pipe_copy(q).wait_recv()
            pltpu.make_async_copy(gin.at[q], pend_hbm.at[q - steps + CHUNKS], e_sem.at[q - steps + CHUNKS]).start()

    for q in range(steps):
        out_copy(q).wait()

        @pl.when(has_next)
        def _(q=q):
            pipe_copy(q).wait_send()

    for d in range(1, n):
        for slot in range(RING):
            scaled_copy(slot, d).wait_send()
            part_copy(slot, d).wait_send()
        for slot in range(min(HELD, steps)):
            act_copy(slot, d).wait_send()
    for c in range(CHUNKS):
        @pl.when(has_prev)
        def _(c=c):
            pltpu.make_async_copy(gin.at[steps - CHUNKS + c], pend_hbm.at[c], e_sem.at[c]).wait()


def shards(n, sections, up_weight, down_weight, norm_gain, layer_scale, stash, slot_order, received, arrivals):
    up_w, down_w = up_weight[0], down_weight[0]
    hid, width = up_w.shape
    _, ticks, tokens, _ = stash.shape
    half = GRID // 2
    lines = tokens // 4 // half
    rows = tokens // CHUNKS
    steps = ticks * CHUNKS
    landed = (
        arrivals.reshape(ticks, lines, half, 2, 2, width)
        .transpose(0, 1, 3, 2, 4, 5)
        .reshape(ticks, tokens, width)
    )
    bf = jnp.bfloat16
    hold = pl.BlockSpec(memory_space=pltpu.VMEM)
    far = pl.BlockSpec(memory_space=pl.ANY)
    dma = pltpu.SemaphoreType.DMA
    tile_count = hid // TILE + (hid % TILE > 0)
    out, pend = pl.pallas_call(
        functools.partial(kernel, n, sections, steps),
        out_shape=(
            jax.ShapeDtypeStruct((steps, rows, width), bf),
            jax.ShapeDtypeStruct((CHUNKS, rows, width), bf),
        ),
        in_specs=[pl.BlockSpec(memory_space=pltpu.SMEM), hold, hold, far, far, far, far, far],
        out_specs=(far, far),
        scratch_shapes=[
            pltpu.VMEM((hid, width), bf),
            pltpu.VMEM((hid, width), bf),
            pltpu.VMEM((ticks, CHUNKS, rows, width), bf),
            pltpu.VMEM((CHUNKS, rows, width), jnp.float32),
            pltpu.VMEM((steps - CHUNKS, rows, width), bf),
            pltpu.VMEM((HELD, n, rows, width), bf),
            pltpu.VMEM((RING, n, rows, width), bf),
            pltpu.VMEM((CHUNKS, n * rows, hid), jnp.float32),
            pltpu.VMEM((n * rows, hid), bf),
            pltpu.VMEM((RING, n, rows, width), bf),
            pltpu.VMEM((RING, n - 1, rows, width), bf),
            pltpu.VMEM((steps, rows, width), bf),
            pltpu.VMEM((steps, rows, width), bf),
            dma((2, tile_count)),
            dma((3,)),
            dma((HELD, n - 1)),
            dma((HELD, n - 1)),
            dma((RING, n - 1)),
            dma((RING, n - 1)),
            dma((RING, n - 1)),
            dma((RING, n - 1)),
            dma((steps,)),
            dma((steps,)),
            dma((steps,)),
            dma((CHUNKS,)),
        ],
        compiler_params=pltpu.CompilerParams(
            collective_id=0, has_side_effects=True, vmem_limit_bytes=67_043_328
        ),
    )(
        slot_order,
        norm_gain,
        layer_scale,
        up_w,
        down_w,
        stash.reshape(ticks, CHUNKS, rows, width),
        received.reshape(CHUNKS, rows, width),
        landed[: ticks - 1].reshape(steps - CHUNKS, rows, width),
    )
    is_last = lax.axis_index("pipe") == sections - 1
    pending = jnp.where(is_last, landed[ticks - 1], pend.reshape(tokens, width)).astype(jnp.float32)
    return out.reshape(1, ticks, tokens, width), pending[None]


def solution(mesh):
    return jax.shard_map(
        functools.partial(shards, mesh.shape["tensor"], mesh.shape["pipe"]),
        mesh=mesh,
        in_specs=(
            P("pipe", "tensor", None),
            P("pipe", "tensor", None),
            P("pipe", None),
            P("pipe", None),
            P("pipe", None, "tensor", None),
            P("pipe", None),
            P("pipe", "tensor", None),
            P(None, "tensor", None),
        ),
        out_specs=(P("pipe", None, "tensor", None), P("pipe", "tensor", None)),
        check_vma=False,
    )
```
